256 devices in a mesh: blk: 8 (over x, z_lo), pair: 32 (over y, z_hi, core).
Axes of the slice: x: 4, y: 4, z: 8 (z_hi: 4, z_lo: 2; z = z_hi * 2 + z_lo), core: 2. Of those that a mesh axis runs over, the one named last changes fastest.
Arguments:
- panels: bfloat16 [192, 384, 4608], P('pair', None, 'blk'), may hold values from -0.875 to 0.875
- pattern: int32 [192, 8], P('pair', 'blk'), may hold values 0 or 1
- point_inverse: float32 [192, 9, 128], P('pair'), as said below
- camera_hessian: float32 [4608, 576], P('blk'), as said below
- damping: int32 [4608], P('blk'), may hold values from 0 to 3
- camera_grad: float32 [4608], P('blk'), may hold values from -6 to 6
- point_grad: float32 [192, 384], P('pair'), may hold values from -6 to 6
Outputs:
- schur: float32 [4608, 4608], P('pair', 'blk')
- reduced_rhs: float32 [4608], P('blk')
The draws below stay inside these ranges and needn't reach their ends.
Inputs may be any that keep to these rules, and one draw needn't show every extreme that they name: point_inverse is symmetric in its 3 x 3 entries with a positive diagonal. camera_hessian blocks are symmetric with a positive diagonal.
All inputs are finite; a program needn't handle non-finite values. No bound on the sum of `pattern` on one device may be relied on, other than what follows from the above.
Results may differ from the reference program's by a relative error of at most 0.003.
Values may be sent and summed in bfloat16 or wider, within the bound.
No kernel may reach another device: no remote copies, remote signals or barrier semaphores. Data moves between devices by JAX's collectives and lax.ppermute only.
A program may use at most 128 MiB of HBM per device.

```python
import jax
import jax.numpy as jnp
from jax import lax

CAMW = 576
PTS = 128
NPB = 192
CAMS = 4608
N_BLK = 8


def draw_point_inverse(key, part):
    key_off = jax.random.fold_in(key, 11)
    key_diag = jax.random.fold_in(key, 12)
    off_raw = jax.random.uniform(key_off, (NPB, 3, 3, PTS), jnp.float32, -0.25, 0.25)
    diag_raw = jnp.exp(jax.random.uniform(key_diag, (NPB, 3, PTS), jnp.float32, jnp.log(0.5), jnp.log(2.0)))
    symmetric = 0.5 * (off_raw + jnp.swapaxes(off_raw, 1, 2))
    eye_mask = jnp.eye(3, dtype=jnp.float32)[None, :, :, None]
    full_matrix = symmetric * (1.0 - eye_mask) + eye_mask * diag_raw[:, :, None, :]
    return full_matrix.reshape(NPB, 9, PTS)


def draw_camera_hessian(key, part):
    key_off = jax.random.fold_in(key, 21)
    key_diag = jax.random.fold_in(key, 22)
    off_raw = 0.05 * jax.random.normal(key_off, (N_BLK, CAMW, CAMW), jnp.float32)
    diag_raw = jnp.exp(jax.random.uniform(key_diag, (N_BLK, CAMW), jnp.float32, 0.0, jnp.log(4.0)))
    symmetric = 0.5 * (off_raw + jnp.swapaxes(off_raw, 1, 2))
    eye_mask = jnp.eye(CAMW, dtype=jnp.float32)[None]
    full_matrix = symmetric * (1.0 - eye_mask) + eye_mask * diag_raw[:, :, None]
    return full_matrix.reshape(CAMS, CAMW)


def plant(entries, key, smallest, top_value):
    longest = entries.shape.index(max(entries.shape))
    spots = []
    for shift in (0, 1):
        where = [jax.random.randint(jax.random.fold_in(key, axis), (), 0, length) for axis, length in enumerate(entries.shape)]
        where[longest] = (where[longest] + shift) % entries.shape[longest]
        spots.append(tuple(where))
    return entries.at[spots[0]].set(smallest).at[spots[1]].set(top_value)


def level_of(own_key, dims, pieces, smallest, largest):
    gain = 1.0
    for dim, shards_of in pieces:
        draws = jax.random.uniform(jax.random.fold_in(jax.random.fold_in(own_key, 6), dim), (shards_of,), jnp.float32, smallest / len(pieces), largest / len(pieces))
        gain = gain * jnp.repeat(jnp.exp(draws), dims[dim] // shards_of).reshape((-1,) + (1,) * (len(dims) - 1 - dim))
    return gain


def bell_draw(rng, shape, width, limit, split=(), kind=jnp.bfloat16):
    entries = width * jax.random.normal(rng, shape, jnp.float32)
    if split:
        entries = entries * level_of(rng, shape, split, -0.22, 0.18)
    return jnp.clip(entries, -limit, limit).astype(kind)


def setup_inputs(seed: int = 0) -> dict:
    key_list = jax.random.split(jax.random.key(seed), 8)
    panels = bell_draw(key_list[0], (NPB, 3 * PTS, CAMS), ((3 * PTS * NPB) ** -0.25), 0.875, ((0, 32), (2, 8)))
    pattern = plant((jax.random.randint(key_list[1], (NPB, N_BLK), 0, 4) < 3).astype(jnp.int32), jax.random.fold_in(key_list[1], 1), 0, 1)
    point_inverse = draw_point_inverse(jax.random.fold_in(key_list[7], 71), 0)
    camera_hessian = draw_camera_hessian(jax.random.fold_in(key_list[7], 71), 0)
    damping = plant(jax.random.randint(key_list[4], (CAMS,), 0, 4), jax.random.fold_in(key_list[4], 1), 0, 3).astype(jnp.int32)
    camera_grad = bell_draw(key_list[5], (CAMS,), 1.0, 6.0, ((0, 8),), jnp.float32)
    point_grad = bell_draw(key_list[6], (NPB, 3 * PTS), 1.0, 6.0, ((0, 32),), jnp.float32)
    return {"panels": panels, "pattern": pattern, "point_inverse": point_inverse, "camera_hessian": camera_hessian, "damping": damping, "camera_grad": camera_grad, "point_grad": point_grad}


def apply_inverse(inverse, shaped):
    parts = []
    for row in range(3):
        total = inverse[:, row * 3, :, None] * shaped[:, 0]
        total = total + inverse[:, row * 3 + 1, :, None] * shaped[:, 1]
        total = total + inverse[:, row * 3 + 2, :, None] * shaped[:, 2]
        parts.append(total)
    return jnp.stack(parts, axis=1)


def reference(panels, pattern, point_inverse, camera_hessian, damping, camera_grad, point_grad):
    observed = jnp.repeat(pattern.astype(jnp.bfloat16), CAMW, axis=1)
    masked = panels * observed[:, None, :]
    shaped = masked.astype(jnp.float32).reshape(NPB, 3, PTS, CAMS)
    scaled = apply_inverse(point_inverse, shaped).astype(jnp.bfloat16).reshape(NPB * 3 * PTS, CAMS)
    flat_panels = masked.reshape(NPB * 3 * PTS, CAMS)
    product = lax.dot_general(scaled, flat_panels, (((0,), (0,)), ((), ())), preferred_element_type=jnp.float32)
    blocks = camera_hessian.reshape(N_BLK, CAMW, CAMW)
    diag_vals = jnp.diagonal(blocks, axis1=1, axis2=2)
    levels = 0.1 * jnp.power(2.0, damping.astype(jnp.float32)).reshape(N_BLK, CAMW)
    damped = blocks + jnp.eye(CAMW, dtype=jnp.float32)[None] * (levels * diag_vals)[:, :, None]
    block_eye = jnp.eye(N_BLK, dtype=jnp.float32)
    placed = block_eye[:, None, :, None] * damped[:, :, None, :]
    schur = placed.reshape(CAMS, CAMS) - product
    grads = point_grad.reshape(NPB, 3, PTS)
    point_step = apply_inverse(point_inverse, grads[:, :, :, None])[..., 0]
    point_step = point_step.astype(jnp.bfloat16).reshape(NPB * 3 * PTS)
    reduced_rhs = camera_grad - jnp.dot(point_step, flat_panels, preferred_element_type=jnp.float32)
    return schur, reduced_rhs
```

```python
import functools

import jax
import jax.numpy as jnp
from jax import lax
from jax.experimental import pallas as pl
from jax.experimental.pallas import tpu as pltpu
from jax.sharding import Mesh
from jax.sharding import PartitionSpec as P

X, L, Y, H, C = 4, 2, 4, 4, 2
BLK = ("x", "l")
PAIR = ("y", "h", "c")
CHUNKS = 3
F32 = jnp.float32
BF16 = jnp.bfloat16


def rotate(array, axis, size, step):
    return lax.ppermute(array, axis, [(i, (i + step) % size) for i in range(size)])


def apply_inverse(inverse, shaped):
    parts = []
    for row in range(3):
        total = inverse[:, row * 3] * shaped[:, 0]
        total = total + inverse[:, row * 3 + 1] * shaped[:, 1]
        total = total + inverse[:, row * 3 + 2] * shaped[:, 2]
        parts.append(total)
    return jnp.stack(parts, axis=1)


def product_kernel(first, last, *refs):
    where_ref, own_ref, mate_ref, next_ref, far_ref, inv_ref = refs[:6]
    refs = refs[6:]
    if not first:
        before_ref, refs = refs[0], refs[1:]
    if last:
        send_ref, keep_ref, scaled_ref, sums_ref = refs
    else:
        sums_ref, scaled_ref = refs
    blocks, width, rows = own_ref.shape
    points = inv_ref.shape[2]
    for block in range(blocks):
        for side, ref in enumerate((own_ref, mate_ref)):
            parts = [
                ref[block, :, c * points : (c + 1) * points].astype(F32) for c in range(3)
            ]
            for a in range(3):
                total = inv_ref[block, 3 * a : 3 * a + 1, :] * parts[0]
                total = total + inv_ref[block, 3 * a + 1 : 3 * a + 2, :] * parts[1]
                total = total + inv_ref[block, 3 * a + 2 : 3 * a + 3, :] * parts[2]
                at = block * rows + a * points
                scaled_ref[side * width : (side + 1) * width, at : at + points] = (
                    total.astype(BF16)
                )
    total_width = 2 * width
    half_start = pl.multiple_of(where_ref[1] * rows, rows)
    for start in range(0, total_width, 256):
        stop = min(start + 256, total_width)
        columns = slice(start, stop)
        for kind in range(3):
            if kind < 2:
                ref = own_ref if kind == 0 else next_ref
                left = jnp.concatenate([ref[b] for b in range(blocks)], axis=1)
                right = scaled_ref[columns, :]
            else:
                left = far_ref[0]
                right = scaled_ref[columns, pl.ds(half_start, rows)]
            term = lax.dot_general(
                left, right, (((1,), (1,)), ((), ())), preferred_element_type=F32
            ).reshape(2, 2, width // 4, stop - start)
            if not first:
                term = term + before_ref[kind, :, :, :, columns]
            if last:
                sums_ref[kind, :, :, :, columns] = term
                core = where_ref[0]
                for i in range(2):
                    send_ref[kind, i, :, columns] = sums_ref[
                        kind, i, 1 - core, :, columns
                    ].astype(BF16)
                    keep_ref[kind, i, :, columns] = sums_ref[
                        kind, i, core, :, columns
                    ].astype(BF16)
            else:
                sums_ref[kind, :, :, :, columns] = term


def product(first, last, where, own, mate, following, far, inverse, before=None):
    blocks, width, rows = own.shape
    sums = (3, 2, 2, width // 4, 2 * width)
    half = (3, 2, width // 4, 2 * width)
    vmem = pl.BlockSpec(memory_space=pltpu.VMEM)
    scaled = pltpu.VMEM((2 * width, blocks * rows), BF16)
    if last:
        out_shape = (jax.ShapeDtypeStruct(half, BF16), jax.ShapeDtypeStruct(half, BF16))
        out_specs = (vmem, vmem)
        scratch = [scaled, pltpu.VMEM(sums, F32)]
    else:
        out_shape = jax.ShapeDtypeStruct(sums, F32)
        out_specs = vmem
        scratch = [scaled]
    operands = [where, own, mate, following, far, inverse]
    specs = [pl.BlockSpec(memory_space=pltpu.SMEM)] + [vmem] * 5
    if not first:
        operands.append(before)
        specs.append(vmem)
    flops = 2 * width * 2 * width * rows * (2 * blocks + 1)
    return pl.pallas_call(
        functools.partial(product_kernel, first, last),
        out_shape=out_shape,
        in_specs=specs,
        out_specs=out_specs,
        scratch_shapes=scratch,
        compiler_params=pltpu.CompilerParams(vmem_limit_bytes=48 * 2**20),
        cost_estimate=pl.CostEstimate(
            flops=flops, bytes_accessed=16 * 2**20, transcendentals=0
        ),
        name="product",
    )(*operands)


def shards(panels, pattern, point_inverse, camera_hessian, damping, camera_grad, point_grad):
    count = panels.shape[0]
    width = panels.shape[2]
    points = point_inverse.shape[2]
    x, l = lax.axis_index("x"), lax.axis_index("l")
    y, h, c = lax.axis_index("y"), lax.axis_index("h"), lax.axis_index("c")
    upper = x // 2
    masked = jnp.transpose(panels, (0, 2, 1)) * pattern.astype(BF16)[:, :, None]

    size = count // CHUNKS
    chunks = []
    for n in range(CHUNKS):
        own = masked[n * size : (n + 1) * size]
        mate = rotate(own, "l", L, 1)
        following = rotate(own, "x", X, -1)
        sent = lax.dynamic_slice_in_dim(masked, n * size + 1 - upper, 1, 0)
        far = rotate(rotate(sent, "x", X, 1), "x", X, 1)
        chunks.append((own, mate, following, far, point_inverse[n * size : (n + 1) * size]))

    grads = point_grad.reshape(count, 3, points)
    step = apply_inverse(point_inverse, grads).astype(BF16).astype(F32)
    step = step.reshape(count, 1, 3 * points)
    terms = jnp.sum(masked.astype(F32) * step, axis=(0, 2))
    terms = terms + rotate(terms, "c", C, 1)
    terms = terms + sum(rotate(terms, "y", Y, k) for k in range(1, Y))
    terms = terms + sum(rotate(terms, "h", H, k) for k in range(1, H))
    reduced_rhs = camera_grad - terms

    where = jnp.stack([c, upper]).astype(jnp.int32)
    sums = None
    for n, chunk in enumerate(chunks):
        sums = product(n == 0, n == CHUNKS - 1, where, *chunk, before=sums)
    send, keep = sums
    other = rotate(send, "c", C, 1)

    def of_kind(kind):
        at = jnp.minimum(kind, 2)
        return lax.dynamic_index_in_dim(keep, at, 0, False).astype(
            F32
        ) + lax.dynamic_index_in_dim(other, at, 0, False).astype(F32)

    kind = (y - x) % Y
    held = jnp.where(kind < 3, of_kind(kind), 0.0)
    for k in range(1, Y):
        pairs = [
            (a * Y + b, a * Y + (b + k) % Y)
            for a in range(X)
            for b in range(Y)
            if (b + k - a) % Y < 3
        ]
        piece = of_kind((y + k - x) % Y).astype(BF16)
        held = held + lax.ppermute(piece, ("x", "y"), pairs).astype(F32)

    pieces = held.reshape(2, width // 4, 2, width)
    total = jnp.zeros((width // 4, width), F32)
    for m in range(4):
        pairs = [
            (a * H + b, ((b ^ m) & 1) * H + 2 * a + ((b ^ m) >> 1))
            for a in range(L)
            for b in range(H)
        ]
        picked = h ^ m
        row = lax.dynamic_index_in_dim(pieces, picked // 2, 0, False)
        side = (picked % 2) ^ l
        piece = jnp.where(side == 0, row[:, 0], row[:, 1]).astype(BF16)
        total = total + lax.ppermute(piece, ("l", "h"), pairs).astype(F32)

    quarter = width // 4
    turned = total.T.reshape(4, quarter, quarter).astype(BF16)
    low = (h % 2) * 2 + c
    mirrored = []
    for m in range(4):
        pairs = []
        for a in range(X):
            for e in range(Y):
                if (e - a) % Y not in (1, 2):
                    continue
                for l0 in range(L):
                    for h0 in range(H):
                        for c0 in range(C):
                            to = ((h0 % 2) * 2 + c0) ^ m
                            source = (((a * L + l0) * Y + e) * H + h0) * C + c0
                            target = (
                                ((e * L + h0 // 2) * Y + a) * H + 2 * l0 + to // 2
                            ) * C + to % 2
                            pairs.append((source, target))
        piece = lax.dynamic_index_in_dim(turned, low ^ m, 0, False)
        mirrored.append(lax.ppermute(piece, ("x", "l", "y", "h", "c"), pairs))
    mirrored = jnp.stack(mirrored)
    mirror = jnp.concatenate(
        [lax.dynamic_index_in_dim(mirrored, low ^ q, 0, False) for q in range(4)], axis=1
    )

    levels = 0.1 * jnp.power(2.0, damping.astype(F32))
    on_diagonal = jnp.eye(width, dtype=bool)
    damped = camera_hessian + jnp.where(on_diagonal, camera_hessian * levels[:, None], 0.0)
    own_rows = lax.dynamic_slice_in_dim(damped, low * quarter, quarter, 0)
    inside = jnp.logical_and(x == y, h // 2 == l)
    schur = jnp.where(inside, own_rows, 0.0) - (total + mirror.astype(F32))
    return (schur, reduced_rhs)


def solution(mesh):
    finer = Mesh(mesh.devices.reshape(X, L, Y, H, C), ("x", "l", "y", "h", "c"))
    in_specs = (
        P(PAIR, None, BLK),
        P(PAIR, BLK),
        P(PAIR, None, None),
        P(BLK, None),
        P(BLK),
        P(BLK),
        P(PAIR, None),
    )
    out_specs = (P(PAIR, BLK), P(BLK))
    return jax.shard_map(
        shards, mesh=finer, in_specs=in_specs, out_specs=out_specs, check_vma=False
    )
```

```python
import functools

import jax
import jax.numpy as jnp
from jax import lax
from jax.experimental import pallas as pl
from jax.experimental.pallas import tpu as pltpu
from jax.sharding import Mesh
from jax.sharding import PartitionSpec as P

X, L, Y, H, C = 4, 2, 4, 4, 2
BLK = ("x", "l")
PAIR = ("y", "h", "c")
CHUNKS = (4, 2)
F32 = jnp.float32
BF16 = jnp.bfloat16


def rotate(array, axis, size, step):
    return lax.ppermute(array, axis, [(i, (i + step) % size) for i in range(size)])


def apply_inverse(inverse, shaped):
    parts = []
    for row in range(3):
        total = inverse[:, row * 3] * shaped[:, 0]
        total = total + inverse[:, row * 3 + 1] * shaped[:, 1]
        total = total + inverse[:, row * 3 + 2] * shaped[:, 2]
        parts.append(total)
    return jnp.stack(parts, axis=1)


def product_kernel(first, last, *refs):
    where_ref, own_ref, mate_ref, next_ref, far_ref, inv_ref = refs[:6]
    refs = refs[6:]
    if not first:
        before_ref, refs = refs[0], refs[1:]
    if last:
        send_ref, keep_ref, scaled_ref, sums_ref = refs
    else:
        sums_ref, scaled_ref = refs
    blocks, width, rows = own_ref.shape
    points = inv_ref.shape[2]
    for block in range(blocks):
        for side, ref in enumerate((own_ref, mate_ref)):
            parts = [
                ref[block, :, c * points : (c + 1) * points].astype(F32) for c in range(3)
            ]
            for a in range(3):
                total = inv_ref[block, 3 * a : 3 * a + 1, :] * parts[0]
                total = total + inv_ref[block, 3 * a + 1 : 3 * a + 2, :] * parts[1]
                total = total + inv_ref[block, 3 * a + 2 : 3 * a + 3, :] * parts[2]
                at = block * rows + a * points
                scaled_ref[side * width : (side + 1) * width, at : at + points] = (
                    total.astype(BF16)
                )
    total_width = 2 * width
    fars = far_ref.shape[0]
    for start in range(0, total_width, 256):
        stop = min(start + 256, total_width)
        columns = slice(start, stop)
        for kind in range(3):
            if kind < 2:
                ref = own_ref if kind == 0 else next_ref
                left = jnp.concatenate([ref[b] for b in range(blocks)], axis=1)
                right = scaled_ref[columns, :]
            else:
                left = jnp.concatenate([far_ref[b] for b in range(fars)], axis=1)
                right = jnp.concatenate(
                    [
                        scaled_ref[
                            columns,
                            pl.ds(pl.multiple_of((2 * b + where_ref[1]) * rows, rows), rows),
                        ]
                        for b in range(fars)
                    ],
                    axis=1,
                )
            term = lax.dot_general(
                left, right, (((1,), (1,)), ((), ())), preferred_element_type=F32
            ).reshape(2, 2, width // 4, stop - start)
            if not first:
                term = term + before_ref[kind, :, :, :, columns]
            if last:
                sums_ref[kind, :, :, :, columns] = term
                core = where_ref[0]
                for i in range(2):
                    send_ref[kind, i, :, columns] = sums_ref[
                        kind, i, 1 - core, :, columns
                    ].astype(BF16)
                    keep_ref[kind, i, :, columns] = sums_ref[
                        kind, i, core, :, columns
                    ].astype(BF16)
            else:
                sums_ref[kind, :, :, :, columns] = term


def product(first, last, where, own, mate, following, far, inverse, before=None):
    blocks, width, rows = own.shape
    sums = (3, 2, 2, width // 4, 2 * width)
    half = (3, 2, width // 4, 2 * width)
    vmem = pl.BlockSpec(memory_space=pltpu.VMEM)
    scaled = pltpu.VMEM((2 * width, blocks * rows), BF16)
    if last:
        out_shape = (jax.ShapeDtypeStruct(half, BF16), jax.ShapeDtypeStruct(half, BF16))
        out_specs = (vmem, vmem)
        scratch = [scaled, pltpu.VMEM(sums, F32)]
    else:
        out_shape = jax.ShapeDtypeStruct(sums, F32)
        out_specs = vmem
        scratch = [scaled]
    operands = [where, own, mate, following, far, inverse]
    specs = [pl.BlockSpec(memory_space=pltpu.SMEM)] + [vmem] * 5
    if not first:
        operands.append(before)
        specs.append(vmem)
    flops = 2 * width * 2 * width * rows * (2 * blocks + far.shape[0])
    return pl.pallas_call(
        functools.partial(product_kernel, first, last),
        out_shape=out_shape,
        in_specs=specs,
        out_specs=out_specs,
        scratch_shapes=scratch,
        compiler_params=pltpu.CompilerParams(vmem_limit_bytes=30 * 2**20),
        cost_estimate=pl.CostEstimate(
            flops=flops, bytes_accessed=16 * 2**20, transcendentals=0
        ),
        name="product",
    )(*operands)


def shards(panels, pattern, point_inverse, camera_hessian, damping, camera_grad, point_grad):
    count = panels.shape[0]
    width = panels.shape[2]
    points = point_inverse.shape[2]
    x, l = lax.axis_index("x"), lax.axis_index("l")
    y, h, c = lax.axis_index("y"), lax.axis_index("h"), lax.axis_index("c")
    upper = x // 2
    masked = jnp.transpose(panels, (0, 2, 1)) * pattern.astype(BF16)[:, :, None]

    sent = jnp.where(
        upper == 0,
        masked.reshape(count // 2, 2, width, 3 * points)[:, 1],
        masked.reshape(count // 2, 2, width, 3 * points)[:, 0],
    )
    chunks = []
    start = 0
    for size in CHUNKS:
        own = masked[start : start + size]
        mate = rotate(own, "l", L, 1)
        following = rotate(own, "x", X, -1)
        far = rotate(sent[start // 2 : (start + size) // 2], "x", X, 1)
        far = rotate(far, "x", X, 1)
        chunks.append([own, mate, following, far, point_inverse[start : start + size]])
        start += size

    grads = point_grad.reshape(count, 3, points)
    step = apply_inverse(point_inverse, grads).astype(BF16).astype(F32)
    step = step.reshape(count, 1, 3 * points)
    terms = jnp.sum(masked.astype(F32) * step, axis=(0, 2))
    terms = terms + rotate(terms, "c", C, 1)
    terms = terms + sum(rotate(terms, "y", Y, k) for k in range(1, Y))
    terms = terms + sum(rotate(terms, "h", H, k) for k in range(1, H))
    reduced_rhs = camera_grad - terms
    reduced_rhs, chunks[0][0] = lax.optimization_barrier((reduced_rhs, chunks[0][0]))

    where = jnp.stack([c, upper]).astype(jnp.int32)
    sums = None
    for n, chunk in enumerate(chunks):
        sums = product(n == 0, n == len(CHUNKS) - 1, where, *chunk, before=sums)
    send, keep = sums
    other = rotate(send, "c", C, 1)

    def of_kind(kind):
        at = jnp.minimum(kind, 2)
        return lax.dynamic_index_in_dim(keep, at, 0, False).astype(
            F32
        ) + lax.dynamic_index_in_dim(other, at, 0, False).astype(F32)

    kind = (y - x) % Y
    held = jnp.where(kind < 3, of_kind(kind), 0.0)
    for k in range(1, Y):
        pairs = [
            (a * Y + b, a * Y + (b + k) % Y)
            for a in range(X)
            for b in range(Y)
            if (b + k - a) % Y < 3
        ]
        piece = of_kind((y + k - x) % Y).astype(BF16)
        held = held + lax.ppermute(piece, ("x", "y"), pairs).astype(F32)

    quarter = width // 4
    total = jnp.zeros((quarter, width), F32)
    for m in range(4):
        pairs = [
            (a * H + b, ((b ^ m) & 1) * H + 2 * a + ((b ^ m) >> 1))
            for a in range(L)
            for b in range(H)
        ]
        picked = h ^ m
        row = jnp.where(picked < 2, held[0], held[1])
        side = (picked % 2) ^ l
        piece = jnp.where(side == 0, row[:, :width], row[:, width:]).astype(BF16)
        total = total + lax.ppermute(piece, ("l", "h"), pairs).astype(F32)

    turned = total.T.reshape(2, 2, quarter, quarter).astype(BF16)
    kept = jnp.where(c == 0, turned[:, 0], turned[:, 1])
    got = rotate(jnp.where(c == 0, turned[:, 1], turned[:, 0]), "c", C, 1)
    turned = jnp.concatenate(
        [jnp.where(c == 0, kept, got), jnp.where(c == 0, got, kept)], axis=2
    )
    mirrored = []
    for m in range(2):
        pairs = []
        for a in range(X):
            for e in range(Y):
                if (e - a) % Y not in (1, 2):
                    continue
                for l0 in range(L):
                    for h0 in range(H):
                        source = ((a * L + l0) * Y + e) * H + h0
                        to = 2 * l0 + (h0 % 2 ^ m)
                        target = ((e * L + h0 // 2) * Y + a) * H + to
                        pairs.append((source, target))
        piece = jnp.where(h % 2 == m, turned[0], turned[1])
        mirrored.append(lax.ppermute(piece, ("x", "l", "y", "h"), pairs))
    even = h % 2 == 0
    mirror = jnp.concatenate(
        [
            jnp.where(even, mirrored[0], mirrored[1]),
            jnp.where(even, mirrored[1], mirrored[0]),
        ],
        axis=1,
    )
    low = (h % 2) * 2 + c

    levels = 0.1 * jnp.power(2.0, damping.astype(F32))
    on_diagonal = jnp.eye(width, dtype=bool)
    damped = camera_hessian + jnp.where(on_diagonal, camera_hessian * levels[:, None], 0.0)
    own_rows = lax.dynamic_slice_in_dim(damped, low * quarter, quarter, 0)
    inside = jnp.logical_and(x == y, h // 2 == l)
    schur = jnp.where(inside, own_rows, 0.0) - (total + mirror.astype(F32))
    return (schur, reduced_rhs)


def solution(mesh):
    finer = Mesh(mesh.devices.reshape(X, L, Y, H, C), ("x", "l", "y", "h", "c"))
    in_specs = (
        P(PAIR, None, BLK),
        P(PAIR, BLK),
        P(PAIR, None, None),
        P(BLK, None),
        P(BLK),
        P(BLK),
        P(PAIR, None),
    )
    out_specs = (P(PAIR, BLK), P(BLK))
    return jax.shard_map(
        shards, mesh=finer, in_specs=in_specs, out_specs=out_specs, check_vma=False
    )
```

```python
import functools

import jax
import jax.numpy as jnp
from jax import lax
from jax.experimental import pallas as pl
from jax.experimental.pallas import tpu as pltpu
from jax.sharding import Mesh
from jax.sharding import PartitionSpec as P

X, L, Y, H, C = 4, 2, 4, 4, 2
BLK = ("x", "l")
PAIR = ("y", "h", "c")
CHUNKS = (4, 2)
F32 = jnp.float32
BF16 = jnp.bfloat16


def rotate(array, axis, size, step):
    return lax.ppermute(array, axis, [(i, (i + step) % size) for i in range(size)])


def small_call(kernel, out_shape, scalars, operands, scratch=()):
    vmem = pl.BlockSpec(memory_space=pltpu.VMEM)
    smem = pl.BlockSpec(memory_space=pltpu.SMEM)
    return pl.pallas_call(
        kernel,
        out_shape=out_shape,
        in_specs=[smem] + [vmem] * len(operands),
        out_specs=jax.tree.map(lambda _: vmem, out_shape),
        scratch_shapes=list(scratch),
        compiler_params=pltpu.CompilerParams(vmem_limit_bytes=24 * 2**20),
        cost_estimate=pl.CostEstimate(flops=10**6, bytes_accessed=2**22, transcendentals=0),
    )(jnp.stack(scalars).astype(jnp.int32), *operands)


def pieces_kernel(which_ref, own_ref, a_ref, b_ref, c_ref, *rest):
    outs, cut_ref = rest[:4], rest[4]
    width = own_ref.shape[2] // 2
    half = width // 2
    for i in range(2):
        total = own_ref[i].astype(F32) + a_ref[i].astype(F32)
        total = total + b_ref[i].astype(F32) + c_ref[i].astype(F32)
        for n in range(4):
            cut_ref[n, :, i * half : (i + 1) * half] = total[:, n * half : (n + 1) * half]
    for m in range(4):
        outs[m][...] = cut_ref[which_ref[m]].astype(BF16)


def turn_kernel(which_ref, *refs):
    ins, (kept_ref, swap_ref, turned_keep_ref, turned_send_ref, turned_ref) = refs[:4], refs[4:]
    quarter, width = ins[0].shape
    half = width // 2
    odd, core = which_ref[0] == 1, which_ref[1]
    wide = ins[0][...].astype(F32) + ins[1][...].astype(F32)
    wide = wide + ins[2][...].astype(F32) + ins[3][...].astype(F32)
    low, high = wide[:, :half], wide[:, half:]
    kept_ref[...] = jnp.where(odd, high, low)
    swap_ref[...] = jnp.where(odd, low, high).astype(BF16)
    shape = (width, width)
    same = lax.broadcasted_iota(jnp.int32, shape, 0) == lax.broadcasted_iota(jnp.int32, shape, 1)
    turned = lax.dot_general(
        same.astype(F32).astype(BF16),
        wide.astype(BF16),
        (((1,), (1,)), ((), ())),
        preferred_element_type=F32,
    )
    turned_ref[...] = turned.reshape(4, quarter, quarter)
    for i in range(2):
        turned_keep_ref[i] = turned_ref[2 * i + core].astype(BF16)
        turned_send_ref[i] = turned_ref[2 * i + 1 - core].astype(BF16)


def last_kernel(which_ref, base_ref, kept_ref, swapped_ref, mirror_ref, out_ref):
    quarter = mirror_ref.shape[2]
    odd = which_ref[0]
    for n in range(4):
        columns = slice((n % 2) * quarter, (n % 2 + 1) * quarter)
        total = jnp.where(
            odd == n // 2, kept_ref[:, columns], swapped_ref[:, columns].astype(F32)
        )
        to = slice(n * quarter, (n + 1) * quarter)
        at = jnp.where(which_ref[1] == n % 2, n // 2, 2 + n // 2)
        out_ref[:, to] = base_ref[:, to] - (total + mirror_ref[at].astype(F32))


def rotate_pairs(array):
    return lax.ppermute(array, "h", [(i, i ^ 1) for i in range(H)])


def apply_inverse(inverse, shaped):
    parts = []
    for row in range(3):
        total = inverse[:, row * 3] * shaped[:, 0]
        total = total + inverse[:, row * 3 + 1] * shaped[:, 1]
        total = total + inverse[:, row * 3 + 2] * shaped[:, 2]
        parts.append(total)
    return jnp.stack(parts, axis=1)


def product_kernel(first, last, at, *refs):
    where_ref, seen_ref, own_ref, mate_ref, next_ref, far_ref, inv_ref = refs[:7]
    refs = refs[7:]
    if not first:
        before_ref, refs = refs[0], refs[1:]
    if last:
        send_ref, keep_ref, left_ref, scaled_ref, sums_ref = refs
    else:
        sums_ref, left_ref, scaled_ref = refs
    blocks, width, rows = own_ref.shape
    points = inv_ref.shape[2]
    fars = far_ref.shape[0]
    core, upper = where_ref[0], where_ref[1]
    for block in range(blocks):
        for side, ref in enumerate((own_ref, mate_ref)):
            seen = seen_ref[side, at + block].astype(F32)
            parts = [
                ref[block, :, c * points : (c + 1) * points].astype(F32) for c in range(3)
            ]
            for a in range(3):
                total = (inv_ref[block, 3 * a : 3 * a + 1, :] * seen) * parts[0]
                total = total + (inv_ref[block, 3 * a + 1 : 3 * a + 2, :] * seen) * parts[1]
                total = total + (inv_ref[block, 3 * a + 2 : 3 * a + 3, :] * seen) * parts[2]
                to = block * rows + a * points
                scaled_ref[side * width : (side + 1) * width, to : to + points] = (
                    total.astype(BF16)
                )
        columns = slice(block * rows, (block + 1) * rows)
        for kind, ref in enumerate((own_ref, next_ref)):
            seen = seen_ref[2 * kind, at + block].astype(F32).astype(BF16)
            left_ref[kind, :, columns] = ref[block] * seen
    for block in range(fars):
        columns = slice(block * rows, (block + 1) * rows)
        seen = seen_ref[3, at + upper * fars + block].astype(F32).astype(BF16)
        left_ref[2, :, columns] = far_ref[block] * seen
    half_start = pl.multiple_of(upper * (fars * rows), rows)
    for start in range(0, 2 * width, 256):
        stop = min(start + 256, 2 * width)
        columns = slice(start, stop)
        for kind in range(3):
            if kind < 2:
                left = left_ref[kind]
                right = scaled_ref[columns, :]
            else:
                left = left_ref[kind, :, : fars * rows]
                right = scaled_ref[columns, pl.ds(half_start, fars * rows)]
            term = lax.dot_general(
                left, right, (((1,), (1,)), ((), ())), preferred_element_type=F32
            ).reshape(2, 2, width // 4, stop - start)
            if not first:
                term = term + before_ref[kind, :, :, :, columns]
            sums_ref[kind, :, :, :, columns] = term
            if last:
                for i in range(2):
                    send_ref[kind, i, :, columns] = sums_ref[
                        kind, i, 1 - core, :, columns
                    ].astype(BF16)
                    keep_ref[kind, i, :, columns] = sums_ref[
                        kind, i, core, :, columns
                    ].astype(BF16)


def product(first, last, at, where, seen, own, mate, following, far, inverse, before=None):
    blocks, width, rows = own.shape
    sums = (3, 2, 2, width // 4, 2 * width)
    half = (3, 2, width // 4, 2 * width)
    vmem = pl.BlockSpec(memory_space=pltpu.VMEM)
    smem = pl.BlockSpec(memory_space=pltpu.SMEM)
    scratch = [
        pltpu.VMEM((3, width, blocks * rows), BF16),
        pltpu.VMEM((2 * width, blocks * rows), BF16),
    ]
    if last:
        out_shape = (jax.ShapeDtypeStruct(half, BF16), jax.ShapeDtypeStruct(half, BF16))
        out_specs = (vmem, vmem)
        scratch.append(pltpu.VMEM(sums, F32))
    else:
        out_shape = jax.ShapeDtypeStruct(sums, F32)
        out_specs = vmem
    operands = [where, seen, own, mate, following, far, inverse]
    specs = [smem, smem] + [vmem] * 5
    if not first:
        operands.append(before)
        specs.append(vmem)
    flops = 2 * width * 2 * width * rows * (2 * blocks + far.shape[0])
    return pl.pallas_call(
        functools.partial(product_kernel, first, last, at),
        out_shape=out_shape,
        in_specs=specs,
        out_specs=out_specs,
        scratch_shapes=scratch,
        compiler_params=pltpu.CompilerParams(vmem_limit_bytes=34 * 2**20),
        cost_estimate=pl.CostEstimate(
            flops=flops, bytes_accessed=16 * 2**20, transcendentals=0
        ),
        name="product",
    )(*operands)


def shards(panels, pattern, point_inverse, camera_hessian, damping, camera_grad, point_grad):
    count = panels.shape[0]
    width = panels.shape[2]
    points = point_inverse.shape[2]
    x, l = lax.axis_index("x"), lax.axis_index("l")
    y, h, c = lax.axis_index("y"), lax.axis_index("h"), lax.axis_index("c")
    upper = x // 2
    raw = jnp.transpose(panels, (0, 2, 1))

    chunks = []
    start = 0
    for size in CHUNKS:
        own = raw[start : start + size]
        half = size // 2
        sent = lax.dynamic_slice_in_dim(raw, start + (1 - upper) * half, half, 0)
        far = rotate(sent, "x", X, 1)
        mate = rotate(own, "l", L, 1)
        following = rotate(own, "x", X, -1)
        chunks.append([start, own, mate, following, far, point_inverse[start : start + size]])
        start += size
    for chunk in chunks:
        chunk[4] = rotate(chunk[4], "x", X, 1)
    seen = pattern[:, 0]
    seen = jnp.stack(
        [seen, rotate(seen, "l", L, 1), rotate(seen, "x", X, -1), rotate(seen, "x", X, 2)]
    )

    grads = point_grad.reshape(count, 3, points)
    step = apply_inverse(point_inverse, grads).astype(BF16).astype(F32)
    step = step.reshape(count, 1, 3 * points)
    masked = raw * pattern.astype(BF16)[:, :, None]
    terms = jnp.sum(masked.astype(F32) * step, axis=(0, 2))
    terms = terms + rotate(terms, "c", C, 1)
    terms = terms + sum(rotate(terms, "y", Y, k) for k in range(1, Y))
    terms, seen = lax.optimization_barrier((terms, seen))

    where = jnp.stack([c, upper]).astype(jnp.int32)
    sums = None
    for n, chunk in enumerate(chunks):
        sums = product(
            n == 0, n == len(CHUNKS) - 1, chunk[0], where, seen, *chunk[1:], before=sums
        )
    send, keep = sums
    other = rotate(send, "c", C, 1)
    terms, keep = lax.optimization_barrier((terms, keep))

    def of_kind(kind):
        at = jnp.minimum(kind, 2)
        return lax.dynamic_index_in_dim(keep, at, 0, False).astype(
            F32
        ) + lax.dynamic_index_in_dim(other, at, 0, False).astype(F32)

    kind = (y - x) % Y
    held = [jnp.where(kind < 3, of_kind(kind), 0.0).astype(BF16)]
    for k in range(1, Y):
        pairs = [
            (a * Y + b, a * Y + (b + k) % Y)
            for a in range(X)
            for b in range(Y)
            if (b + k - a) % Y < 3
        ]
        piece = of_kind((y + k - x) % Y).astype(BF16)
        held.append(lax.ppermute(piece, ("x", "y"), pairs))
    terms = terms + sum(rotate(terms, "h", H, k) for k in range(1, H))
    reduced_rhs = camera_grad - terms
    reduced_rhs, held[0] = lax.optimization_barrier((reduced_rhs, held[0]))

    quarter = width // 4
    picked = [h ^ m for m in range(4)]
    piece_shape = jax.ShapeDtypeStruct((quarter, width), BF16)
    pieces = small_call(
        pieces_kernel,
        [piece_shape] * 4,
        [((p % 2) ^ l) * 2 + p // 2 for p in picked],
        held,
        [pltpu.VMEM((4, quarter, width), F32)],
    )
    came = []
    for m in range(4):
        pairs = [
            (a * H + b, ((b ^ m) & 1) * H + 2 * a + ((b ^ m) >> 1))
            for a in range(L)
            for b in range(H)
        ]
        came.append(lax.ppermute(pieces[m], ("l", "h"), pairs))

    half_shape = (quarter, width // 2)
    tile_shape = jax.ShapeDtypeStruct((2, quarter, quarter), BF16)
    kept, swap, turned_keep, turned_send = small_call(
        turn_kernel,
        [
            jax.ShapeDtypeStruct(half_shape, F32),
            jax.ShapeDtypeStruct(half_shape, BF16),
            tile_shape,
            tile_shape,
        ],
        [h % 2, c],
        came,
        [pltpu.VMEM((4, quarter, quarter), F32)],
    )
    got = rotate(turned_send, "c", C, 1)
    swapped = rotate_pairs(swap)
    parts = jnp.concatenate([turned_keep, got], axis=0)
    pairs = []
    for a in range(X):
        for e in range(Y):
            if (e - a) % Y not in (1, 2):
                continue
            for l0 in range(L):
                for h0 in range(H):
                    source = ((a * L + l0) * Y + e) * H + h0
                    target = ((e * L + h0 // 2) * Y + a) * H + 2 * l0 + h0 % 2
                    pairs.append((source, target))
    mirror = lax.ppermute(parts, ("x", "l", "y", "h"), pairs)
    low = (h % 2) * 2 + c

    levels = 0.1 * jnp.power(2.0, damping.astype(F32))
    on_diagonal = jnp.eye(width, dtype=bool)
    damped = camera_hessian + jnp.where(on_diagonal, camera_hessian * levels[:, None], 0.0)
    own_rows = lax.dynamic_slice_in_dim(damped, low * quarter, quarter, 0)
    inside = jnp.logical_and(x == y, h // 2 == l)
    base = jnp.where(inside, own_rows, 0.0)
    schur = small_call(
        last_kernel,
        jax.ShapeDtypeStruct((quarter, width), F32),
        [h % 2, c],
        [base, kept, swapped, mirror],
        (),
    )
    return (schur, reduced_rhs)


def solution(mesh):
    finer = Mesh(mesh.devices.reshape(X, L, Y, H, C), ("x", "l", "y", "h", "c"))
    in_specs = (
        P(PAIR, None, BLK),
        P(PAIR, BLK),
        P(PAIR, None, None),
        P(BLK, None),
        P(BLK),
        P(BLK),
        P(PAIR, None),
    )
    out_specs = (P(PAIR, BLK), P(BLK))
    return jax.shard_map(
        shards, mesh=finer, in_specs=in_specs, out_specs=out_specs, check_vma=False
    )
```

```python
import functools

import jax
import jax.numpy as jnp
from jax import lax
from jax.experimental import pallas as pl
from jax.experimental.pallas import tpu as pltpu
from jax.sharding import Mesh
from jax.sharding import PartitionSpec as P

X, L, Y, H, C = 4, 2, 4, 4, 2
BLK = ("x", "l")
PAIR = ("y", "h", "c")
CHUNKS = (4, 2)
F32 = jnp.float32
BF16 = jnp.bfloat16


def rotate(array, axis, size, step):
    return lax.ppermute(array, axis, [(i, (i + step) % size) for i in range(size)])


def small_call(kernel, out_shape, scalars, operands, scratch=()):
    vmem = pl.BlockSpec(memory_space=pltpu.VMEM)
    smem = pl.BlockSpec(memory_space=pltpu.SMEM)
    return pl.pallas_call(
        kernel,
        out_shape=out_shape,
        in_specs=[smem] + [vmem] * len(operands),
        out_specs=jax.tree.map(lambda _: vmem, out_shape),
        scratch_shapes=list(scratch),
        compiler_params=pltpu.CompilerParams(vmem_limit_bytes=24 * 2**20),
        cost_estimate=pl.CostEstimate(flops=10**6, bytes_accessed=2**22, transcendentals=0),
    )(jnp.stack(scalars).astype(jnp.int32), *operands)


def pieces_kernel(which_ref, own_ref, a_ref, b_ref, c_ref, *rest):
    outs, cut_ref = rest[:4], rest[4]
    quarter, width = own_ref.shape
    half, rows = width // 4, quarter // 2
    total = own_ref[...].astype(F32) + a_ref[...].astype(F32)
    total = total + b_ref[...].astype(F32) + c_ref[...].astype(F32)
    for n in range(4):
        for p in range(2):
            cut_ref[n, :, p * half : (p + 1) * half] = total[
                p * rows : (p + 1) * rows, n * half : (n + 1) * half
            ]
    for m in range(4):
        outs[m][...] = cut_ref[which_ref[m]].astype(BF16)


def turn_kernel(which_ref, *refs):
    ins = refs[:8]
    kept_ref, swap_ref, turned_keep_ref, turned_send_ref, wide_ref, turned_ref = refs[8:]
    rows, width = ins[0].shape
    half, quarter = width // 2, 2 * rows
    odd, core = which_ref[0], which_ref[1]
    for i in range(2):
        total = ins[4 * i][...].astype(F32) + ins[4 * i + 1][...].astype(F32)
        total = total + ins[4 * i + 2][...].astype(F32) + ins[4 * i + 3][...].astype(F32)
        for p in range(2):
            wide_ref[i, p * rows : (p + 1) * rows, :] = total[:, p * half : (p + 1) * half]
    kept_ref[...] = wide_ref[odd]
    other = wide_ref[1 - odd].astype(BF16)
    for p in range(2):
        swap_ref[:, p * half : (p + 1) * half] = other[p * rows : (p + 1) * rows]
    shape = (half, half)
    same = lax.broadcasted_iota(jnp.int32, shape, 0) == lax.broadcasted_iota(jnp.int32, shape, 1)
    same = same.astype(F32).astype(BF16)
    for i in range(2):
        turned = lax.dot_general(
            same, wide_ref[i].astype(BF16), (((1,), (1,)), ((), ())), preferred_element_type=F32
        )
        turned_ref[...] = turned.reshape(2, quarter, quarter)
        turned_keep_ref[i] = turned_ref[core].astype(BF16)
        turned_send_ref[i] = turned_ref[1 - core].astype(BF16)


def pack_kernel(which_ref, keep_ref, got_ref, out_ref):
    del which_ref
    quarter = keep_ref.shape[1]
    for n in range(4):
        ref = keep_ref if n < 2 else got_ref
        out_ref[:, n * quarter : (n + 1) * quarter] = ref[n % 2]


def last_kernel(which_ref, base_ref, kept_ref, swapped_ref, mirror_ref, out_ref, full_ref):
    quarter, half = kept_ref.shape
    rows = quarter // 2
    odd, core = which_ref[0], which_ref[1]
    for p in range(2):
        full_ref[p * rows : (p + 1) * rows, :] = swapped_ref[
            :, p * half : (p + 1) * half
        ].astype(F32)
    for n in range(4):
        columns = slice((n % 2) * quarter, (n % 2 + 1) * quarter)
        total = jnp.where(odd == n // 2, kept_ref[:, columns], full_ref[:, columns])
        at, other = n // 2, 2 + n // 2
        mirror = jnp.where(
            core == n % 2,
            mirror_ref[:, at * quarter : (at + 1) * quarter].astype(F32),
            mirror_ref[:, other * quarter : (other + 1) * quarter].astype(F32),
        )
        to = slice(n * quarter, (n + 1) * quarter)
        out_ref[:, to] = base_ref[:, to] - (total + mirror)


def rotate_pairs(array):
    return lax.ppermute(array, "h", [(i, i ^ 1) for i in range(H)])


def apply_inverse(inverse, shaped):
    parts = []
    for row in range(3):
        total = inverse[:, row * 3] * shaped[:, 0]
        total = total + inverse[:, row * 3 + 1] * shaped[:, 1]
        total = total + inverse[:, row * 3 + 2] * shaped[:, 2]
        parts.append(total)
    return jnp.stack(parts, axis=1)


def product_kernel(first, last, at, *refs):
    where_ref, seen_ref, own_ref, mate_ref, next_ref, far_ref, inv_ref = refs[:7]
    refs = refs[7:]
    if not first:
        before_ref, refs = refs[0], refs[1:]
    if last:
        sends, keeps, (left_ref, scaled_ref, sums_ref) = refs[:2], refs[2:4], refs[4:]
    else:
        sums_ref, left_ref, scaled_ref = refs
    blocks, width, rows = own_ref.shape
    points = inv_ref.shape[2]
    fars = far_ref.shape[0]
    core, upper = where_ref[0], where_ref[1]
    for block in range(blocks):
        for side, ref in enumerate((own_ref, mate_ref)):
            seen = seen_ref[side, at + block].astype(F32)
            parts = [
                ref[block, :, c * points : (c + 1) * points].astype(F32) for c in range(3)
            ]
            for a in range(3):
                total = (inv_ref[block, 3 * a : 3 * a + 1, :] * seen) * parts[0]
                total = total + (inv_ref[block, 3 * a + 1 : 3 * a + 2, :] * seen) * parts[1]
                total = total + (inv_ref[block, 3 * a + 2 : 3 * a + 3, :] * seen) * parts[2]
                to = block * rows + a * points
                scaled_ref[side * width : (side + 1) * width, to : to + points] = (
                    total.astype(BF16)
                )
        columns = slice(block * rows, (block + 1) * rows)
        for kind, ref in enumerate((own_ref, next_ref)):
            seen = seen_ref[2 * kind, at + block].astype(F32).astype(BF16)
            left_ref[kind, :, columns] = ref[block] * seen
    for block in range(fars):
        columns = slice(block * rows, (block + 1) * rows)
        seen = seen_ref[3, at + upper * fars + block].astype(F32).astype(BF16)
        left_ref[2, :, columns] = far_ref[block] * seen
    half_start = pl.multiple_of(upper * (fars * rows), rows)
    for start in range(0, 2 * width, 256):
        stop = min(start + 256, 2 * width)
        columns = slice(start, stop)
        for kind in range(3):
            if kind < 2:
                left = left_ref[kind]
                right = scaled_ref[columns, :]
            else:
                left = left_ref[kind, :, : fars * rows]
                right = scaled_ref[columns, pl.ds(half_start, fars * rows)]
            term = lax.dot_general(
                left, right, (((1,), (1,)), ((), ())), preferred_element_type=F32
            ).reshape(2, 2, width // 4, stop - start)
            if not first:
                term = term + before_ref[kind, :, :, :, columns]
            sums_ref[kind, :, :, :, columns] = term
            if last:
                for i in range(2):
                    sends[i][kind, :, columns] = sums_ref[
                        kind, i, 1 - core, :, columns
                    ].astype(BF16)
                    keeps[i][kind, :, columns] = sums_ref[
                        kind, i, core, :, columns
                    ].astype(BF16)


def product(first, last, at, where, seen, own, mate, following, far, inverse, before=None):
    blocks, width, rows = own.shape
    sums = (3, 2, 2, width // 4, 2 * width)
    half = (3, width // 4, 2 * width)
    vmem = pl.BlockSpec(memory_space=pltpu.VMEM)
    smem = pl.BlockSpec(memory_space=pltpu.SMEM)
    scratch = [
        pltpu.VMEM((3, width, blocks * rows), BF16),
        pltpu.VMEM((2 * width, blocks * rows), BF16),
    ]
    if last:
        out_shape = [jax.ShapeDtypeStruct(half, BF16)] * 4
        out_specs = [vmem] * 4
        scratch.append(pltpu.VMEM(sums, F32))
    else:
        out_shape = jax.ShapeDtypeStruct(sums, F32)
        out_specs = vmem
    operands = [where, seen, own, mate, following, far, inverse]
    specs = [smem, smem] + [vmem] * 5
    if not first:
        operands.append(before)
        specs.append(vmem)
    flops = 2 * width * 2 * width * rows * (2 * blocks + far.shape[0])
    return pl.pallas_call(
        functools.partial(product_kernel, first, last, at),
        out_shape=out_shape,
        in_specs=specs,
        out_specs=out_specs,
        scratch_shapes=scratch,
        compiler_params=pltpu.CompilerParams(vmem_limit_bytes=34 * 2**20),
        cost_estimate=pl.CostEstimate(
            flops=flops, bytes_accessed=16 * 2**20, transcendentals=0
        ),
        name="product",
    )(*operands)


def shards(panels, pattern, point_inverse, camera_hessian, damping, camera_grad, point_grad):
    count = panels.shape[0]
    width = panels.shape[2]
    points = point_inverse.shape[2]
    x, l = lax.axis_index("x"), lax.axis_index("l")
    y, h, c = lax.axis_index("y"), lax.axis_index("h"), lax.axis_index("c")
    upper = x // 2
    raw = jnp.transpose(panels, (0, 2, 1))

    chunks = []
    start = 0
    for size in CHUNKS:
        own = raw[start : start + size]
        half = size // 2
        sent = lax.dynamic_slice_in_dim(raw, start + (1 - upper) * half, half, 0)
        far = rotate(sent, "x", X, 1)
        mate = rotate(own, "l", L, 1)
        following = rotate(own, "x", X, -1)
        chunks.append([start, own, mate, following, far, point_inverse[start : start + size]])
        start += size
    for chunk in chunks:
        chunk[4] = rotate(chunk[4], "x", X, 1)
    seen = pattern[:, 0]
    seen = jnp.stack(
        [seen, rotate(seen, "l", L, 1), rotate(seen, "x", X, -1), rotate(seen, "x", X, 2)]
    )

    grads = point_grad.reshape(count, 3, points)
    step = apply_inverse(point_inverse, grads).astype(BF16).astype(F32)
    step = step.reshape(count, 1, 3 * points)
    masked = raw * pattern.astype(BF16)[:, :, None]
    terms = jnp.sum(masked.astype(F32) * step, axis=(0, 2))
    terms = terms + rotate(terms, "c", C, 1)
    terms = terms + sum(rotate(terms, "y", Y, k) for k in range(1, Y))
    terms, seen = lax.optimization_barrier((terms, seen))

    where = jnp.stack([c, upper]).astype(jnp.int32)
    sums = None
    for n, chunk in enumerate(chunks):
        sums = product(
            n == 0, n == len(CHUNKS) - 1, chunk[0], where, seen, *chunk[1:], before=sums
        )
    sends, keeps = sums[:2], list(sums[2:])
    others = []
    for i in range(2):
        others.append(rotate(sends[i], "c", C, 1))

    kind = (y - x) % Y
    held = []
    for i in range(2):

        def of_kind(kind):
            at = jnp.minimum(kind, 2)
            return lax.dynamic_index_in_dim(keeps[i], at, 0, False).astype(
                F32
            ) + lax.dynamic_index_in_dim(others[i], at, 0, False).astype(F32)

        parts = [jnp.where(kind < 3, of_kind(kind), 0.0).astype(BF16)]
        for k in range(1, Y):
            pairs = [
                (a * Y + b, a * Y + (b + k) % Y)
                for a in range(X)
                for b in range(Y)
                if (b + k - a) % Y < 3
            ]
            piece = of_kind((y + k - x) % Y).astype(BF16)
            if i == 0 and k == Y - 1:
                terms, piece = lax.optimization_barrier((terms, piece))
            parts.append(lax.ppermute(piece, ("x", "y"), pairs))
        held.append(parts)
    terms = terms + sum(rotate(terms, "h", H, k) for k in range(1, H))
    reduced_rhs = camera_grad - terms
    reduced_rhs, held[1][0] = lax.optimization_barrier((reduced_rhs, held[1][0]))

    quarter = width // 4
    picked = [h ^ m for m in range(4)]
    piece_shape = jax.ShapeDtypeStruct((quarter // 2, width), BF16)
    came = []
    for i in range(2):
        pieces = small_call(
            pieces_kernel,
            [piece_shape] * 4,
            [((p % 2) ^ l) * 2 + p // 2 for p in picked],
            held[i],
            [pltpu.VMEM((4, quarter // 2, width), F32)],
        )
        for m in range(4):
            pairs = [
                (a * H + b, ((b ^ m) & 1) * H + 2 * a + ((b ^ m) >> 1))
                for a in range(L)
                for b in range(H)
            ]
            came.append(lax.ppermute(pieces[m], ("l", "h"), pairs))

    half_shape = (quarter, width // 2)
    tile_shape = jax.ShapeDtypeStruct((2, quarter, quarter), BF16)
    kept, swap, turned_keep, turned_send = small_call(
        turn_kernel,
        [
            jax.ShapeDtypeStruct(half_shape, F32),
            piece_shape,
            tile_shape,
            tile_shape,
        ],
        [h % 2, c],
        came,
        [pltpu.VMEM((2, *half_shape), F32), pltpu.VMEM((2, quarter, quarter), F32)],
    )
    got = rotate(turned_send, "c", C, 1)
    swapped = rotate_pairs(swap)
    mirrored = small_call(
        pack_kernel, jax.ShapeDtypeStruct((quarter, width), BF16), [c], [turned_keep, got], ()
    )
    pairs = []
    for a in range(X):
        for e in range(Y):
            if (e - a) % Y not in (1, 2):
                continue
            for l0 in range(L):
                for h0 in range(H):
                    source = ((a * L + l0) * Y + e) * H + h0
                    target = ((e * L + h0 // 2) * Y + a) * H + 2 * l0 + h0 % 2
                    pairs.append((source, target))
    mirror = lax.ppermute(mirrored, ("x", "l", "y", "h"), pairs)
    low = (h % 2) * 2 + c

    levels = 0.1 * jnp.power(2.0, damping.astype(F32))
    on_diagonal = jnp.eye(width, dtype=bool)
    damped = camera_hessian + jnp.where(on_diagonal, camera_hessian * levels[:, None], 0.0)
    own_rows = lax.dynamic_slice_in_dim(damped, low * quarter, quarter, 0)
    inside = jnp.logical_and(x == y, h // 2 == l)
    base = jnp.where(inside, own_rows, 0.0)
    schur = small_call(
        last_kernel,
        jax.ShapeDtypeStruct((quarter, width), F32),
        [h % 2, c],
        [base, kept, swapped, mirror],
        [pltpu.VMEM(half_shape, F32)],
    )
    return (schur, reduced_rhs)


def solution(mesh):
    finer = Mesh(mesh.devices.reshape(X, L, Y, H, C), ("x", "l", "y", "h", "c"))
    in_specs = (
        P(PAIR, None, BLK),
        P(PAIR, BLK),
        P(PAIR, None, None),
        P(BLK, None),
        P(BLK),
        P(BLK),
        P(PAIR, None),
    )
    out_specs = (P(PAIR, BLK), P(BLK))
    return jax.shard_map(
        shards, mesh=finer, in_specs=in_specs, out_specs=out_specs, check_vma=False
    )
```

```python
import functools

import jax
import jax.numpy as jnp
from jax import lax
from jax.experimental import pallas as pl
from jax.experimental.pallas import tpu as pltpu
from jax.sharding import Mesh
from jax.sharding import PartitionSpec as P


X, L, Y, H, C = 4, 2, 4, 4, 2
BLK = ("x", "l")
PAIR = ("y", "h", "c")
CHUNKS = (4, 2)
F32 = jnp.float32
BF16 = jnp.bfloat16


def rotate(array, axis, size, step):
    return lax.ppermute(array, axis, [(i, (i + step) % size) for i in range(size)])


def small_call(kernel, out_shape, scalars, operands, scratch=()):
    vmem = pl.BlockSpec(memory_space=pltpu.VMEM)
    smem = pl.BlockSpec(memory_space=pltpu.SMEM)
    return pl.pallas_call(
        kernel,
        out_shape=out_shape,
        in_specs=[smem] + [vmem] * len(operands),
        out_specs=jax.tree.map(lambda _: vmem, out_shape),
        scratch_shapes=list(scratch),
        compiler_params=pltpu.CompilerParams(vmem_limit_bytes=24 * 2**20),
        cost_estimate=pl.CostEstimate(flops=10**6, bytes_accessed=2**22, transcendentals=0),
    )(jnp.stack(scalars).astype(jnp.int32), *operands)


def pieces_kernel(which_ref, *refs):
    halves, terms_ref, outs, cut_ref = (refs[:4], refs[4:8]), refs[8], refs[9:13], refs[13]
    quarter, width = halves[0][0].shape
    half, rows = width // 4, quarter // 2
    for i, parts in enumerate(halves):
        total = parts[0][...].astype(F32) + parts[1][...].astype(F32)
        total = total + parts[2][...].astype(F32) + parts[3][...].astype(F32)
        for n in range(4):
            for p in range(2):
                cut_ref[n, i * rows : (i + 1) * rows, p * half : (p + 1) * half] = total[
                    p * rows : (p + 1) * rows, n * half : (n + 1) * half
                ]
    for m in range(4):
        outs[m][:quarter] = cut_ref[which_ref[m]].astype(BF16)
        more = outs[m].shape[0] - quarter
        term = terms_ref[pl.ds(which_ref[4 + m], 1), :]
        high = term.astype(BF16).astype(F32)
        row = lax.broadcasted_iota(jnp.int32, (more, width // 2), 0)
        both = jnp.where(row == 0, high, jnp.where(row == 1, term - high, 0.0))
        outs[m][quarter:] = both.astype(BF16)


def turn_kernel(which_ref, *refs):
    ins = refs[:4]
    kept_ref, swap_ref, turned_keep_ref, turned_send_ref, terms_ref = refs[4:9]
    wide_ref, turned_ref = refs[9:]
    quarter, half = kept_ref.shape
    rows = quarter // 2
    odd, core = which_ref[0], which_ref[1]
    total = ins[0][...].astype(F32) + ins[1][...].astype(F32)
    total = total + ins[2][...].astype(F32) + ins[3][...].astype(F32)
    for i in range(2):
        for p in range(2):
            wide_ref[i, p * rows : (p + 1) * rows, :] = total[
                i * rows : (i + 1) * rows, p * half : (p + 1) * half
            ]
    terms_ref[...] = total[quarter:]
    kept_ref[...] = wide_ref[odd]
    other = wide_ref[1 - odd].astype(BF16)
    for p in range(2):
        swap_ref[:, p * half : (p + 1) * half] = other[p * rows : (p + 1) * rows]
    shape = (half, half)
    same = lax.broadcasted_iota(jnp.int32, shape, 0) == lax.broadcasted_iota(jnp.int32, shape, 1)
    same = same.astype(F32).astype(BF16)
    for i in range(2):
        turned = lax.dot_general(
            same, wide_ref[i].astype(BF16), (((1,), (1,)), ((), ())), preferred_element_type=F32
        )
        turned_ref[...] = turned.reshape(2, quarter, quarter)
        turned_keep_ref[i] = turned_ref[core].astype(BF16)
        turned_send_ref[i] = turned_ref[1 - core].astype(BF16)


def pack_kernel(which_ref, keep_ref, got_ref, out_ref):
    del which_ref
    quarter = keep_ref.shape[1]
    for n in range(4):
        ref = keep_ref if n < 2 else got_ref
        out_ref[:, n * quarter : (n + 1) * quarter] = ref[n % 2]


def last_kernel(which_ref, base_ref, kept_ref, swapped_ref, mirror_ref, out_ref, full_ref):
    quarter, half = kept_ref.shape
    rows = quarter // 2
    odd, core = which_ref[0], which_ref[1]
    for p in range(2):
        full_ref[p * rows : (p + 1) * rows, :] = swapped_ref[
            :, p * half : (p + 1) * half
        ].astype(F32)
    for n in range(4):
        columns = slice((n % 2) * quarter, (n % 2 + 1) * quarter)
        total = jnp.where(odd == n // 2, kept_ref[:, columns], full_ref[:, columns])
        at, other = n // 2, 2 + n // 2
        mirror = jnp.where(
            core == n % 2,
            mirror_ref[:, at * quarter : (at + 1) * quarter].astype(F32),
            mirror_ref[:, other * quarter : (other + 1) * quarter].astype(F32),
        )
        to = slice(n * quarter, (n + 1) * quarter)
        out_ref[:, to] = base_ref[:, to] - (total + mirror)


def rotate_pairs(array):
    return lax.ppermute(array, "h", [(i, i ^ 1) for i in range(H)])


def apply_inverse(inverse, shaped):
    parts = []
    for row in range(3):
        total = inverse[:, row * 3] * shaped[:, 0]
        total = total + inverse[:, row * 3 + 1] * shaped[:, 1]
        total = total + inverse[:, row * 3 + 2] * shaped[:, 2]
        parts.append(total)
    return jnp.stack(parts, axis=1)


def product_kernel(first, last, at, *refs):
    where_ref, seen_ref, own_ref, mate_ref, next_ref, far_ref, inv_ref = refs[:7]
    refs = refs[7:]
    if not first:
        before_ref, refs = refs[0], refs[1:]
    if last:
        sends, keeps, refs = refs[:2], refs[2:4], refs[4:]
        sums_ref, refs = refs[-1], refs[:-1]
    else:
        sums_ref, refs = refs[0], refs[1:]
    left_ref, scaled_ref, mate_here, next_here, arrived = refs
    loads = [
        pltpu.make_async_copy(mate_ref, mate_here, arrived.at[0]),
        pltpu.make_async_copy(next_ref, next_here, arrived.at[1]),
    ]
    for load in loads:
        load.start()
    blocks, width, rows = own_ref.shape
    points = inv_ref.shape[2]
    fars = far_ref.shape[0]
    core, upper = where_ref[0], where_ref[1]

    def scale(side, ref):
        for block in range(blocks):
            seen = seen_ref[side, at + block].astype(F32)
            parts = [
                ref[block, :, c * points : (c + 1) * points].astype(F32) for c in range(3)
            ]
            for a in range(3):
                total = (inv_ref[block, 3 * a : 3 * a + 1, :] * seen) * parts[0]
                total = total + (inv_ref[block, 3 * a + 1 : 3 * a + 2, :] * seen) * parts[1]
                total = total + (inv_ref[block, 3 * a + 2 : 3 * a + 3, :] * seen) * parts[2]
                to = block * rows + a * points
                scaled_ref[side * width : (side + 1) * width, to : to + points] = (
                    total.astype(BF16)
                )

    def place(kind, ref, row, shift):
        for block in range(ref.shape[0]):
            seen = seen_ref[row, at + shift + block].astype(F32).astype(BF16)
            left_ref[kind, :, block * rows : (block + 1) * rows] = ref[block] * seen

    scale(0, own_ref)
    place(0, own_ref, 0, 0)
    place(2, far_ref, 3, upper * fars)
    loads[0].wait()
    scale(1, mate_here)
    loads[1].wait()
    place(1, next_here, 2, 0)
    half_start = pl.multiple_of(upper * (fars * rows), rows)
    for start in range(0, 2 * width, 256):
        stop = min(start + 256, 2 * width)
        columns = slice(start, stop)
        for kind in range(3):
            if kind < 2:
                left = left_ref[kind]
                right = scaled_ref[columns, :]
            else:
                left = left_ref[kind, :, : fars * rows]
                right = scaled_ref[columns, pl.ds(half_start, fars * rows)]
            term = lax.dot_general(
                left, right, (((1,), (1,)), ((), ())), preferred_element_type=F32
            ).reshape(2, 2, width // 4, stop - start)
            if not first:
                term = term + before_ref[kind, :, :, :, columns]
            if last:
                wide = stop - start
                sums_ref[:, :, :, :wide] = term
                for i in range(2):
                    sends[i][kind, :, columns] = sums_ref[i, 1 - core, :, :wide].astype(BF16)
                    keeps[i][kind, :, columns] = sums_ref[i, core, :, :wide].astype(BF16)
            else:
                sums_ref[kind, :, :, :, columns] = term


def product(first, last, at, where, seen, own, mate, following, far, inverse, before=None):
    blocks, width, rows = own.shape
    sums = (3, 2, 2, width // 4, 2 * width)
    half = (3, width // 4, 2 * width)
    vmem = pl.BlockSpec(memory_space=pltpu.VMEM)
    smem = pl.BlockSpec(memory_space=pltpu.SMEM)
    scratch = [
        pltpu.VMEM((3, width, blocks * rows), BF16),
        pltpu.VMEM((2 * width, blocks * rows), BF16),
        pltpu.VMEM(own.shape, BF16),
        pltpu.VMEM(own.shape, BF16),
        pltpu.SemaphoreType.DMA((2,)),
    ]
    if last:
        out_shape = [jax.ShapeDtypeStruct(half, BF16)] * 4
        out_specs = [vmem] * 4
        scratch.append(pltpu.VMEM((2, 2, width // 4, 256), F32))
    else:
        out_shape = jax.ShapeDtypeStruct(sums, F32)
        out_specs = vmem
    operands = [where, seen, own, mate, following, far, inverse]
    specs = [smem, smem, vmem, pl.BlockSpec(memory_space=pltpu.HBM)]
    specs += [pl.BlockSpec(memory_space=pltpu.HBM), vmem, vmem]
    if not first:
        operands.append(before)
        specs.append(vmem)
    flops = 2 * width * 2 * width * rows * (2 * blocks + far.shape[0])
    return pl.pallas_call(
        functools.partial(product_kernel, first, last, at),
        out_shape=out_shape,
        in_specs=specs,
        out_specs=out_specs,
        scratch_shapes=scratch,
        compiler_params=pltpu.CompilerParams(vmem_limit_bytes=(18 if last else 28) * 2**20),
        cost_estimate=pl.CostEstimate(
            flops=flops, bytes_accessed=16 * 2**20, transcendentals=0
        ),
        name="product",
    )(*operands)


def shards(panels, pattern, point_inverse, camera_hessian, damping, camera_grad, point_grad):
    count = panels.shape[0]
    width = panels.shape[2]
    points = point_inverse.shape[2]
    x, l = lax.axis_index("x"), lax.axis_index("l")
    y, h, c = lax.axis_index("y"), lax.axis_index("h"), lax.axis_index("c")
    upper = x // 2
    raw = jnp.transpose(panels, (0, 2, 1))

    chunks = []
    start = 0
    for size in CHUNKS:
        own = raw[start : start + size]
        half = size // 2
        sent = lax.dynamic_slice_in_dim(raw, start + (1 - upper) * half, half, 0)
        far = rotate(sent, "x", X, 1)
        mate = rotate(own, "l", L, 1)
        following = rotate(own, "x", X, -1)
        chunks.append([start, own, mate, following, far, point_inverse[start : start + size]])
        start += size
    for chunk in chunks:
        chunk[4] = rotate(chunk[4], "x", X, 1)
    seen = pattern[:, 0]
    seen = jnp.stack(
        [seen, rotate(seen, "l", L, 1), rotate(seen, "x", X, -1), rotate(seen, "x", X, 2)]
    )

    grads = point_grad.reshape(count, 3, points)
    step = apply_inverse(point_inverse, grads).astype(BF16).astype(F32)
    step = step.reshape(count, 1, 3 * points)
    masked = raw * pattern.astype(BF16)[:, :, None]
    terms = jnp.sum(masked.astype(F32) * step, axis=(0, 2))
    terms = terms + rotate(terms, "c", C, 1)
    terms = terms + sum(rotate(terms, "y", Y, k) for k in range(1, Y))
    terms, seen = lax.optimization_barrier((terms, seen))

    where = jnp.stack([c, upper]).astype(jnp.int32)
    sums = None
    for n, chunk in enumerate(chunks):
        sums = product(
            n == 0, n == len(CHUNKS) - 1, chunk[0], where, seen, *chunk[1:], before=sums
        )
    sends, keeps = sums[:2], list(sums[2:])
    terms, keeps[0] = lax.optimization_barrier((terms, keeps[0]))
    across = rotate(terms, "l", L, 1)
    terms = jnp.stack([jnp.where(l == 0, terms, across), jnp.where(l == 0, across, terms)])
    others = []
    for i in range(2):
        others.append(rotate(sends[i], "c", C, 1))

    kind = (y - x) % Y
    held = []
    for i in range(2):

        def of_kind(kind):
            at = jnp.minimum(kind, 2)
            return lax.dynamic_index_in_dim(keeps[i], at, 0, False).astype(
                F32
            ) + lax.dynamic_index_in_dim(others[i], at, 0, False).astype(F32)

        parts = [jnp.where(kind < 3, of_kind(kind), 0.0).astype(BF16)]
        for k in range(1, Y):
            pairs = [
                (a * Y + b, a * Y + (b + k) % Y)
                for a in range(X)
                for b in range(Y)
                if (b + k - a) % Y < 3
            ]
            piece = of_kind((y + k - x) % Y).astype(BF16)
            parts.append(lax.ppermute(piece, ("x", "y"), pairs))
        held.append(parts)
    quarter = width // 4
    picked = [h ^ m for m in range(4)]
    piece_shape = jax.ShapeDtypeStruct((quarter // 2, width), BF16)
    pieces = small_call(
        pieces_kernel,
        [jax.ShapeDtypeStruct((quarter + 8, width), BF16)] * 4,
        [((p % 2) ^ l) * 2 + p // 2 for p in picked] + [p % 2 for p in picked],
        held[0] + held[1] + [terms],
        [pltpu.VMEM((4, quarter, width), F32)],
    )
    came = []
    for m in range(4):
        pairs = [
            (a * H + b, ((b ^ m) & 1) * H + 2 * a + ((b ^ m) >> 1))
            for a in range(L)
            for b in range(H)
        ]
        came.append(lax.ppermute(pieces[m], ("l", "h"), pairs))

    half_shape = (quarter, width // 2)
    tile_shape = jax.ShapeDtypeStruct((2, quarter, quarter), BF16)
    kept, swap, turned_keep, turned_send, terms = small_call(
        turn_kernel,
        [
            jax.ShapeDtypeStruct(half_shape, F32),
            piece_shape,
            tile_shape,
            tile_shape,
            jax.ShapeDtypeStruct((8, width), F32),
        ],
        [h % 2, c],
        came,
        [pltpu.VMEM((2, *half_shape), F32), pltpu.VMEM((2, quarter, quarter), F32)],
    )
    reduced_rhs = camera_grad - (terms[0] + terms[1])
    got = rotate(turned_send, "c", C, 1)
    swapped = rotate_pairs(swap)
    mirrored = small_call(
        pack_kernel, jax.ShapeDtypeStruct((quarter, width), BF16), [c], [turned_keep, got], ()
    )
    pairs = []
    for a in range(X):
        for e in range(Y):
            if (e - a) % Y not in (1, 2):
                continue
            for l0 in range(L):
                for h0 in range(H):
                    source = ((a * L + l0) * Y + e) * H + h0
                    target = ((e * L + h0 // 2) * Y + a) * H + 2 * l0 + h0 % 2
                    pairs.append((source, target))
    mirror = lax.ppermute(mirrored, ("x", "l", "y", "h"), pairs)
    low = (h % 2) * 2 + c

    levels = 0.1 * jnp.power(2.0, damping.astype(F32))
    on_diagonal = jnp.eye(width, dtype=bool)
    damped = camera_hessian + jnp.where(on_diagonal, camera_hessian * levels[:, None], 0.0)
    own_rows = lax.dynamic_slice_in_dim(damped, low * quarter, quarter, 0)
    inside = jnp.logical_and(x == y, h // 2 == l)
    base = jnp.where(inside, own_rows, 0.0)
    schur = small_call(
        last_kernel,
        jax.ShapeDtypeStruct((quarter, width), F32),
        [h % 2, c],
        [base, kept, swapped, mirror],
        [pltpu.VMEM(half_shape, F32)],
    )
    return (schur, reduced_rhs)


def solution(mesh):
    finer = Mesh(mesh.devices.reshape(X, L, Y, H, C), ("x", "l", "y", "h", "c"))
    in_specs = (
        P(PAIR, None, BLK),
        P(PAIR, BLK),
        P(PAIR, None, None),
        P(BLK, None),
        P(BLK),
        P(BLK),
        P(PAIR, None),
    )
    out_specs = (P(PAIR, BLK), P(BLK))
    return jax.shard_map(
        shards, mesh=finer, in_specs=in_specs, out_specs=out_specs, check_vma=False
    )
```

```python
import functools

import jax
import jax.numpy as jnp
from jax import lax
from jax.experimental import pallas as pl
from jax.experimental.pallas import tpu as pltpu
from jax.sharding import Mesh
from jax.sharding import PartitionSpec as P


X, L, Y, H, C = 4, 2, 4, 4, 2
BLK = ("x", "l")
PAIR = ("y", "h", "c")
CHUNKS = (2, 2, 2)
F32 = jnp.float32
BF16 = jnp.bfloat16


def rotate(array, axis, size, step):
    return lax.ppermute(array, axis, [(i, (i + step) % size) for i in range(size)])


def small_call(kernel, out_shape, scalars, operands, scratch=()):
    vmem = pl.BlockSpec(memory_space=pltpu.VMEM)
    smem = pl.BlockSpec(memory_space=pltpu.SMEM)
    return pl.pallas_call(
        kernel,
        out_shape=out_shape,
        in_specs=[smem] + [vmem] * len(operands),
        out_specs=jax.tree.map(lambda _: vmem, out_shape),
        scratch_shapes=list(scratch),
        compiler_params=pltpu.CompilerParams(vmem_limit_bytes=24 * 2**20),
        cost_estimate=pl.CostEstimate(flops=10**6, bytes_accessed=2**22, transcendentals=0),
    )(jnp.stack(scalars).astype(jnp.int32), *operands)


def pieces_kernel(which_ref, own_ref, a_ref, b_ref, c_ref, terms_ref, *rest):
    outs, cut_ref = rest[:4], rest[4]
    quarter, width = own_ref.shape
    half, rows = width // 4, quarter // 2
    total = own_ref[...].astype(F32) + a_ref[...].astype(F32)
    total = total + b_ref[...].astype(F32) + c_ref[...].astype(F32)
    for n in range(4):
        for p in range(2):
            cut_ref[n, :, p * half : (p + 1) * half] = total[
                p * rows : (p + 1) * rows, n * half : (n + 1) * half
            ]
    for m in range(4):
        outs[m][:rows] = cut_ref[which_ref[m]].astype(BF16)
        more = outs[m].shape[0] - rows
        if more:
            term = terms_ref[pl.ds(which_ref[4 + m], 1), :]
            high = term.astype(BF16).astype(F32)
            row = lax.broadcasted_iota(jnp.int32, (more, width // 2), 0)
            both = jnp.where(row == 0, high, jnp.where(row == 1, term - high, 0.0))
            outs[m][rows:] = both.astype(BF16)


def turn_kernel(which_ref, *refs):
    ins = refs[:8]
    kept_ref, swap_ref, turned_keep_ref, turned_send_ref, terms_ref = refs[8:13]
    wide_ref, turned_ref = refs[13:]
    rows, width = ins[4].shape
    half, quarter = width // 2, 2 * rows
    odd, core = which_ref[0], which_ref[1]
    for i in range(2):
        total = ins[4 * i][...].astype(F32) + ins[4 * i + 1][...].astype(F32)
        total = total + ins[4 * i + 2][...].astype(F32) + ins[4 * i + 3][...].astype(F32)
        for p in range(2):
            wide_ref[i, p * rows : (p + 1) * rows, :] = total[
                :rows, p * half : (p + 1) * half
            ]
        if i == 0:
            terms_ref[...] = total[rows:]
    kept_ref[...] = wide_ref[odd]
    other = wide_ref[1 - odd].astype(BF16)
    for p in range(2):
        swap_ref[:, p * half : (p + 1) * half] = other[p * rows : (p + 1) * rows]
    shape = (half, half)
    same = lax.broadcasted_iota(jnp.int32, shape, 0) == lax.broadcasted_iota(jnp.int32, shape, 1)
    same = same.astype(F32).astype(BF16)
    for i in range(2):
        turned = lax.dot_general(
            same, wide_ref[i].astype(BF16), (((1,), (1,)), ((), ())), preferred_element_type=F32
        )
        turned_ref[...] = turned.reshape(2, quarter, quarter)
        turned_keep_ref[i] = turned_ref[core].astype(BF16)
        turned_send_ref[i] = turned_ref[1 - core].astype(BF16)


def pack_kernel(which_ref, keep_ref, got_ref, out_ref):
    del which_ref
    quarter = keep_ref.shape[1]
    for n in range(4):
        ref = keep_ref if n < 2 else got_ref
        out_ref[:, n * quarter : (n + 1) * quarter] = ref[n % 2]


def last_kernel(which_ref, base_ref, kept_ref, swapped_ref, mirror_ref, out_ref, full_ref):
    quarter, half = kept_ref.shape
    rows = quarter // 2
    odd, core = which_ref[0], which_ref[1]
    for p in range(2):
        full_ref[p * rows : (p + 1) * rows, :] = swapped_ref[
            :, p * half : (p + 1) * half
        ].astype(F32)
    for n in range(4):
        columns = slice((n % 2) * quarter, (n % 2 + 1) * quarter)
        total = jnp.where(odd == n // 2, kept_ref[:, columns], full_ref[:, columns])
        at, other = n // 2, 2 + n // 2
        mirror = jnp.where(
            core == n % 2,
            mirror_ref[:, at * quarter : (at + 1) * quarter].astype(F32),
            mirror_ref[:, other * quarter : (other + 1) * quarter].astype(F32),
        )
        to = slice(n * quarter, (n + 1) * quarter)
        out_ref[:, to] = base_ref[:, to] - (total + mirror)


def rotate_pairs(array):
    return lax.ppermute(array, "h", [(i, i ^ 1) for i in range(H)])


def apply_inverse(inverse, shaped):
    parts = []
    for row in range(3):
        total = inverse[:, row * 3] * shaped[:, 0]
        total = total + inverse[:, row * 3 + 1] * shaped[:, 1]
        total = total + inverse[:, row * 3 + 2] * shaped[:, 2]
        parts.append(total)
    return jnp.stack(parts, axis=1)


def product_kernel(first, last, at, *refs):
    where_ref, seen_ref, own_ref, mate_ref, next_ref, far_ref, inv_ref = refs[:7]
    refs = refs[7:]
    if not first:
        before_ref, refs = refs[0], refs[1:]
    if last:
        sends, keeps, refs = refs[:2], refs[2:4], refs[4:]
        sums_ref, refs = refs[-1], refs[:-1]
    else:
        sums_ref, refs = refs[0], refs[1:]
    left_ref, scaled_ref, mate_here, next_here, arrived = refs
    loads = [
        pltpu.make_async_copy(mate_ref, mate_here, arrived.at[0]),
        pltpu.make_async_copy(next_ref, next_here, arrived.at[1]),
    ]
    for load in loads:
        load.start()
    blocks, width, rows = own_ref.shape
    points = inv_ref.shape[2]
    fars = far_ref.shape[0]
    core, upper = where_ref[0], where_ref[1]

    def scale(side, ref):
        for block in range(blocks):
            seen = seen_ref[side, at + block].astype(F32)
            parts = [
                ref[block, :, c * points : (c + 1) * points].astype(F32) for c in range(3)
            ]
            for a in range(3):
                total = (inv_ref[block, 3 * a : 3 * a + 1, :] * seen) * parts[0]
                total = total + (inv_ref[block, 3 * a + 1 : 3 * a + 2, :] * seen) * parts[1]
                total = total + (inv_ref[block, 3 * a + 2 : 3 * a + 3, :] * seen) * parts[2]
                to = block * rows + a * points
                scaled_ref[side * width : (side + 1) * width, to : to + points] = (
                    total.astype(BF16)
                )

    def place(kind, ref, row, shift):
        for block in range(ref.shape[0]):
            seen = seen_ref[row, at + shift + block].astype(F32).astype(BF16)
            left_ref[kind, :, block * rows : (block + 1) * rows] = ref[block] * seen

    scale(0, own_ref)
    place(0, own_ref, 0, 0)
    place(2, far_ref, 3, upper * fars)
    loads[0].wait()
    scale(1, mate_here)
    loads[1].wait()
    place(1, next_here, 2, 0)
    half_start = pl.multiple_of(upper * (fars * rows), rows)
    for start in range(0, 2 * width, 256):
        stop = min(start + 256, 2 * width)
        columns = slice(start, stop)
        for kind in range(3):
            if kind < 2:
                left = left_ref[kind]
                right = scaled_ref[columns, :]
            else:
                left = left_ref[kind, :, : fars * rows]
                right = scaled_ref[columns, pl.ds(half_start, fars * rows)]
            term = lax.dot_general(
                left, right, (((1,), (1,)), ((), ())), preferred_element_type=F32
            ).reshape(2, 2, width // 4, stop - start)
            if not first:
                term = term + before_ref[kind, :, :, :, columns]
            if last:
                wide = stop - start
                sums_ref[:, :, :, :wide] = term
                for i in range(2):
                    sends[i][kind, :, columns] = sums_ref[i, 1 - core, :, :wide].astype(BF16)
                    keeps[i][kind, :, columns] = sums_ref[i, core, :, :wide].astype(BF16)
            else:
                sums_ref[kind, :, :, :, columns] = term


def product(first, last, at, where, seen, own, mate, following, far, inverse, before=None):
    blocks, width, rows = own.shape
    sums = (3, 2, 2, width // 4, 2 * width)
    half = (3, width // 4, 2 * width)
    vmem = pl.BlockSpec(memory_space=pltpu.VMEM)
    smem = pl.BlockSpec(memory_space=pltpu.SMEM)
    scratch = [
        pltpu.VMEM((3, width, blocks * rows), BF16),
        pltpu.VMEM((2 * width, blocks * rows), BF16),
        pltpu.VMEM(own.shape, BF16),
        pltpu.VMEM(own.shape, BF16),
        pltpu.SemaphoreType.DMA((2,)),
    ]
    if last:
        out_shape = [jax.ShapeDtypeStruct(half, BF16)] * 4
        out_specs = [vmem] * 4
        scratch.append(pltpu.VMEM((2, 2, width // 4, 256), F32))
    else:
        out_shape = jax.ShapeDtypeStruct(sums, F32)
        out_specs = vmem
    operands = [where, seen, own, mate, following, far, inverse]
    specs = [smem, smem, vmem, pl.BlockSpec(memory_space=pltpu.HBM)]
    specs += [pl.BlockSpec(memory_space=pltpu.HBM), vmem, vmem]
    if not first:
        operands.append(before)
        specs.append(vmem)
    flops = 2 * width * 2 * width * rows * (2 * blocks + far.shape[0])
    return pl.pallas_call(
        functools.partial(product_kernel, first, last, at),
        out_shape=out_shape,
        in_specs=specs,
        out_specs=out_specs,
        scratch_shapes=scratch,
        compiler_params=pltpu.CompilerParams(vmem_limit_bytes=(18 if last else 28) * 2**20),
        cost_estimate=pl.CostEstimate(
            flops=flops, bytes_accessed=16 * 2**20, transcendentals=0
        ),
        name="product",
    )(*operands)


def shards(panels, pattern, point_inverse, camera_hessian, damping, camera_grad, point_grad):
    count = panels.shape[0]
    width = panels.shape[2]
    points = point_inverse.shape[2]
    x, l = lax.axis_index("x"), lax.axis_index("l")
    y, h, c = lax.axis_index("y"), lax.axis_index("h"), lax.axis_index("c")
    upper = x // 2
    raw = jnp.transpose(panels, (0, 2, 1))

    chunks = []
    start = 0
    for size in CHUNKS:
        own = raw[start : start + size]
        half = size // 2
        sent = lax.dynamic_slice_in_dim(raw, start + (1 - upper) * half, half, 0)
        far = rotate(sent, "x", X, 1)
        mate = rotate(own, "l", L, 1)
        following = rotate(own, "x", X, -1)
        chunks.append([start, own, mate, following, far, point_inverse[start : start + size]])
        start += size
    for chunk in chunks:
        chunk[4] = rotate(chunk[4], "x", X, 1)
    seen = pattern[:, 0]
    seen = jnp.stack(
        [seen, rotate(seen, "l", L, 1), rotate(seen, "x", X, -1), rotate(seen, "x", X, 2)]
    )

    grads = point_grad.reshape(count, 3, points)
    step = apply_inverse(point_inverse, grads).astype(BF16).astype(F32)
    step = step.reshape(count, 1, 3 * points)
    masked = raw * pattern.astype(BF16)[:, :, None]
    terms = jnp.sum(masked.astype(F32) * step, axis=(0, 2))
    terms = terms + rotate(terms, "c", C, 1)
    terms = terms + sum(rotate(terms, "y", Y, k) for k in range(1, Y))
    terms, seen = lax.optimization_barrier((terms, seen))

    where = jnp.stack([c, upper]).astype(jnp.int32)
    sums = None
    for n, chunk in enumerate(chunks):
        sums = product(
            n == 0, n == len(CHUNKS) - 1, chunk[0], where, seen, *chunk[1:], before=sums
        )
    sends, keeps = sums[:2], list(sums[2:])
    terms, keeps[0] = lax.optimization_barrier((terms, keeps[0]))
    across = rotate(terms, "l", L, 1)
    terms = jnp.stack([jnp.where(l == 0, terms, across), jnp.where(l == 0, across, terms)])
    others = []
    for i in range(2):
        others.append(rotate(sends[i], "c", C, 1))

    kind = (y - x) % Y
    held = []
    for i in range(2):

        def of_kind(kind):
            at = jnp.minimum(kind, 2)
            return lax.dynamic_index_in_dim(keeps[i], at, 0, False).astype(
                F32
            ) + lax.dynamic_index_in_dim(others[i], at, 0, False).astype(F32)

        parts = [jnp.where(kind < 3, of_kind(kind), 0.0).astype(BF16)]
        for k in range(1, Y):
            pairs = [
                (a * Y + b, a * Y + (b + k) % Y)
                for a in range(X)
                for b in range(Y)
                if (b + k - a) % Y < 3
            ]
            piece = of_kind((y + k - x) % Y).astype(BF16)
            parts.append(lax.ppermute(piece, ("x", "y"), pairs))
        held.append(parts)
    quarter = width // 4
    picked = [h ^ m for m in range(4)]
    piece_shape = jax.ShapeDtypeStruct((quarter // 2, width), BF16)
    first_shape = jax.ShapeDtypeStruct((quarter // 2 + 8, width), BF16)
    came = []
    for i in range(2):
        pieces = small_call(
            pieces_kernel,
            [first_shape if i == 0 else piece_shape] * 4,
            [((p % 2) ^ l) * 2 + p // 2 for p in picked] + [p % 2 for p in picked],
            held[i] + [terms],
            [pltpu.VMEM((4, quarter // 2, width), F32)],
        )
        for m in range(4):
            pairs = [
                (a * H + b, ((b ^ m) & 1) * H + 2 * a + ((b ^ m) >> 1))
                for a in range(L)
                for b in range(H)
            ]
            came.append(lax.ppermute(pieces[m], ("l", "h"), pairs))

    half_shape = (quarter, width // 2)
    tile_shape = jax.ShapeDtypeStruct((2, quarter, quarter), BF16)
    kept, swap, turned_keep, turned_send, terms = small_call(
        turn_kernel,
        [
            jax.ShapeDtypeStruct(half_shape, F32),
            piece_shape,
            tile_shape,
            tile_shape,
            jax.ShapeDtypeStruct((8, width), F32),
        ],
        [h % 2, c],
        came,
        [pltpu.VMEM((2, *half_shape), F32), pltpu.VMEM((2, quarter, quarter), F32)],
    )
    reduced_rhs = camera_grad - (terms[0] + terms[1])
    got = rotate(turned_send, "c", C, 1)
    swapped = rotate_pairs(swap)
    mirrored = small_call(
        pack_kernel, jax.ShapeDtypeStruct((quarter, width), BF16), [c], [turned_keep, got], ()
    )
    pairs = []
    for a in range(X):
        for e in range(Y):
            if (e - a) % Y not in (1, 2):
                continue
            for l0 in range(L):
                for h0 in range(H):
                    source = ((a * L + l0) * Y + e) * H + h0
                    target = ((e * L + h0 // 2) * Y + a) * H + 2 * l0 + h0 % 2
                    pairs.append((source, target))
    mirror = lax.ppermute(mirrored, ("x", "l", "y", "h"), pairs)
    low = (h % 2) * 2 + c

    levels = 0.1 * jnp.power(2.0, damping.astype(F32))
    on_diagonal = jnp.eye(width, dtype=bool)
    damped = camera_hessian + jnp.where(on_diagonal, camera_hessian * levels[:, None], 0.0)
    own_rows = lax.dynamic_slice_in_dim(damped, low * quarter, quarter, 0)
    inside = jnp.logical_and(x == y, h // 2 == l)
    base = jnp.where(inside, own_rows, 0.0)
    schur = small_call(
        last_kernel,
        jax.ShapeDtypeStruct((quarter, width), F32),
        [h % 2, c],
        [base, kept, swapped, mirror],
        [pltpu.VMEM(half_shape, F32)],
    )
    return (schur, reduced_rhs)


def solution(mesh):
    finer = Mesh(mesh.devices.reshape(X, L, Y, H, C), ("x", "l", "y", "h", "c"))
    in_specs = (
        P(PAIR, None, BLK),
        P(PAIR, BLK),
        P(PAIR, None, None),
        P(BLK, None),
        P(BLK),
        P(BLK),
        P(PAIR, None),
    )
    out_specs = (P(PAIR, BLK), P(BLK))
    return jax.shard_map(
        shards, mesh=finer, in_specs=in_specs, out_specs=out_specs, check_vma=False
    )
```
